512 devices in a mesh: ctx: 128 (over z, y, core), head: 4 (over x).
Axes of the slice: x: 4, y: 8, z: 8, core: 2. Of those that a mesh axis runs over, the one named last changes fastest.
Arguments:
- queries: bfloat16 [49152, 8, 128], P('ctx', 'head'), may hold values from -6 to 6
- key_rows: bfloat16 [49152, 128], P('ctx'), may hold values from -6 to 6
- value_rows: bfloat16 [49152, 128], P('ctx'), may hold values from -6 to 6
- grad_out: bfloat16 [49152, 8, 128], P('ctx', 'head'), may hold values from -6 to 6
- doc_lengths: int32 [64], replicated, may hold values from 1 to 36864, as said below
- block_pattern: int32 [384, 384], P('ctx'), may hold values from 0 to 1, as said below
Outputs:
- attn_out: bfloat16 [49152, 8, 128], P('ctx', 'head')
- grad_queries: bfloat16 [49152, 8, 128], P('ctx', 'head')
- grad_keys: bfloat16 [49152, 128], P('ctx')
- grad_values: bfloat16 [49152, 128], P('ctx')
The draws below stay inside these ranges and needn't reach their ends.
Inputs may be any that keep to these rules, and one draw needn't show every extreme that they name: block_pattern[i, j] is 0 unless i // 3 - j // 3 is 0 or a positive power of two; it is 1 where i == j. `doc_lengths`: the lengths sum to 49152; the first document has exactly 36864 positions.
All inputs are finite; a program needn't handle non-finite values.
Results may differ from the reference program's by a relative error of at most 0.017.
Values may be sent and summed in bfloat16 or wider, within the bound.
No kernel may reach another device: no remote copies, remote signals or barrier semaphores. Data moves between devices by JAX's collectives and lax.ppermute only.
A program may use at most 64 MiB of HBM per device.

```python
import math
import jax
import jax.numpy as jnp
from jax import lax

HEADS = 8
DH = 128
TOK_DEV = 384
BLOCK = 128
DOCS = 64
TOKENS = 49152
BLK_DEV = 3
NBLK = 384
LEVELS = 7
N_CTX = 128


def draw_queries(key, part):
    noise = jnp.clip(jax.random.normal(jax.random.fold_in(key, 1), (TOKENS, HEADS, DH), jnp.float32), -6.0, 6.0)
    return noise.astype(jnp.bfloat16)


def draw_key_rows(key, part):
    noise = jnp.clip(jax.random.normal(jax.random.fold_in(key, 2), (TOKENS, DH), jnp.float32), -6.0, 6.0)
    return noise.astype(jnp.bfloat16)


def draw_doc_lengths(key, part):
    rest_total = TOKENS - 3 * TOKENS // 4
    order = jax.random.permutation(jax.random.fold_in(key, 5), rest_total - 1)
    cuts = jnp.sort(order[:DOCS - 2] + 1).astype(jnp.int32)
    edges = jnp.concatenate([jnp.zeros((1,), jnp.int32), cuts, jnp.full((1,), rest_total, jnp.int32)])
    rest_lengths = (edges[1:] - edges[:-1]).astype(jnp.int32)
    return jnp.concatenate([jnp.full((1,), 3 * TOKENS // 4, jnp.int32), rest_lengths]).astype(jnp.int32)


def draw_block_pattern(key, part):
    block_ids = jnp.arange(NBLK, dtype=jnp.int32)
    shard_gap = block_ids[:, None] // BLK_DEV - block_ids[None, :] // BLK_DEV
    allowed = (shard_gap >= 0) & (jnp.bitwise_and(shard_gap, shard_gap - 1) == 0)
    kept = jax.random.randint(jax.random.fold_in(key, 3), (NBLK, NBLK), 0, 4) != 0
    diagonal = block_ids[:, None] == block_ids[None, :]
    return jnp.where(allowed & (kept | diagonal), 1, 0).astype(jnp.int32)


def level_of(rng, shape, split, least, high):
    gain, own = 1.0, jax.random.fold_in(rng, 6)
    for dim, shards_of in split:
        heights = jnp.exp(jax.random.uniform(jax.random.fold_in(own, dim), (shards_of,), jnp.float32, least / len(split), high / len(split)))
        gain = gain * jnp.repeat(heights, shape[dim] // shards_of).reshape([-1 if axis == dim else 1 for axis in range(len(shape))])
    return gain


def gaussian(rng, extent, width, bound, split=(), kind=jnp.bfloat16):
    level = level_of(rng, extent, split, -0.22, 0.18) if split else 1.0
    result = jax.random.normal(rng, extent, jnp.float32) * width * level
    return jnp.minimum(jnp.maximum(result, -bound), bound).astype(kind)


def setup_inputs(seed: int = 0) -> dict:
    keys = jax.random.split(jax.random.key(seed), 7)
    queries = draw_queries(jax.random.fold_in(keys[6], 71), 0)
    key_rows = draw_key_rows(jax.random.fold_in(keys[6], 71), 0)
    value_rows = gaussian(keys[2], (TOKENS, DH), 1.0, 6.0, ((0, 128),))
    grad_out = gaussian(keys[3], (TOKENS, HEADS, DH), 1.0, 6.0, ((0, 128), (1, 4)))
    doc_lengths = draw_doc_lengths(jax.random.fold_in(keys[6], 71), 0)
    block_pattern = draw_block_pattern(jax.random.fold_in(keys[6], 71), 0)
    return {"queries": queries, "key_rows": key_rows, "value_rows": value_rows, "grad_out": grad_out, "doc_lengths": doc_lengths, "block_pattern": block_pattern}


NEG_FILL = -1e+30

def doc_index(doc_lengths, positions):
    doc_ends = jnp.cumsum(doc_lengths, dtype=jnp.int32)
    return lax.optimization_barrier(jnp.sum((doc_ends[None, :] <= positions[:, None]).astype(jnp.int32), axis=1))

def pair_mask(pattern_rows, query_shard, key_shard, doc_lengths):
    offsets = jnp.arange(TOK_DEV, dtype=jnp.int32)
    query_pos = query_shard * TOK_DEV + offsets
    key_pos = key_shard * TOK_DEV + offsets
    blocks_live = lax.dynamic_slice_in_dim(pattern_rows, (key_shard * BLK_DEV).astype(jnp.int32), BLK_DEV, 1)
    blocks_live = jnp.repeat(jnp.repeat(blocks_live, BLOCK, axis=0), BLOCK, axis=1)
    same_doc = doc_index(doc_lengths, query_pos)[:, None] == doc_index(doc_lengths, key_pos)[None, :]
    return (blocks_live == 1) & same_doc & (key_pos[None, :] <= query_pos[:, None])

def to_low(array):
    return lax.optimization_barrier(array.astype(jnp.bfloat16)).astype(jnp.float32)

def reference(queries, key_rows, value_rows, grad_out, doc_lengths, block_pattern):
    score_scale = 1.0 / math.sqrt(DH)

    def shard_step(carried, query_shard):
        keys_grad, values_grad = carried
        row_start = (query_shard * TOK_DEV).astype(jnp.int32)
        q_rows = lax.dynamic_slice_in_dim(queries, row_start, TOK_DEV, 0).astype(jnp.float32)
        out_grad = lax.dynamic_slice_in_dim(grad_out, row_start, TOK_DEV, 0).astype(jnp.float32)
        pattern_rows = lax.dynamic_slice_in_dim(block_pattern, (query_shard * BLK_DEV).astype(jnp.int32), BLK_DEV, 0)
        raw_partners = [query_shard] + [query_shard - jnp.int32(1 << bit_index) for bit_index in range(LEVELS)]
        partners = [jnp.maximum(item, 0).astype(jnp.int32) for item in raw_partners]
        valid_list = [item >= 0 for item in raw_partners]
        key_list = []
        value_list = []
        mask_list = []
        score_list = []
        for partner, valid in zip(partners, valid_list):
            key_start = (partner * TOK_DEV).astype(jnp.int32)
            key_here = lax.dynamic_slice_in_dim(key_rows, key_start, TOK_DEV, 0).astype(jnp.float32)
            value_here = lax.dynamic_slice_in_dim(value_rows, key_start, TOK_DEV, 0).astype(jnp.float32)
            live_mask = pair_mask(pattern_rows, query_shard, partner, doc_lengths) & valid
            raw_scores = jnp.einsum('thd,ud->htu', q_rows, key_here) * score_scale
            key_list.append(key_here)
            value_list.append(value_here)
            mask_list.append(live_mask)
            score_list.append(jnp.where(live_mask[None], raw_scores, NEG_FILL))
        row_max = score_list[0].max(axis=-1)
        for scores in score_list[1:]:
            row_max = jnp.maximum(row_max, scores.max(axis=-1))
        row_total = jnp.zeros_like(row_max)
        for scores, live_mask in zip(score_list, mask_list):
            row_total = row_total + lax.optimization_barrier(jnp.sum(jnp.where(live_mask[None], jnp.exp(scores - row_max[..., None]), 0.0), axis=-1))
        prob_list = []
        out_acc = jnp.zeros((TOK_DEV, HEADS, DH), jnp.float32)
        for scores, live_mask, value_here in zip(score_list, mask_list, value_list):
            probs = jnp.where(live_mask[None], jnp.exp(scores - row_max[..., None]) / row_total[..., None], 0.0)
            prob_list.append(probs)
            out_acc = out_acc + jnp.einsum('htu,ud->thd', to_low(probs), value_here)
        attn_rows = out_acc.astype(jnp.bfloat16)
        out_dot = lax.optimization_barrier(jnp.sum(out_grad * attn_rows.astype(jnp.float32), axis=-1)).T
        query_grad = jnp.zeros((TOK_DEV, HEADS, DH), jnp.float32)
        for partner, probs, key_here, value_here in zip(partners, prob_list, key_list, value_list):
            grad_prob = jnp.einsum('thd,ud->htu', out_grad, value_here)
            grad_score = to_low(probs * (grad_prob - out_dot[..., None]) * score_scale)
            query_grad = query_grad + jnp.einsum('htu,ud->thd', grad_score, key_here)
            part_key = jnp.einsum('htu,thd->ud', grad_score, q_rows)
            part_value = jnp.einsum('htu,thd->ud', to_low(probs), out_grad)
            key_start = (partner * TOK_DEV).astype(jnp.int32)
            keys_grad = lax.dynamic_update_slice_in_dim(keys_grad, lax.dynamic_slice_in_dim(keys_grad, key_start, TOK_DEV, 0) + part_key, key_start, 0)
            values_grad = lax.dynamic_update_slice_in_dim(values_grad, lax.dynamic_slice_in_dim(values_grad, key_start, TOK_DEV, 0) + part_value, key_start, 0)
        return ((keys_grad, values_grad), (attn_rows, query_grad.astype(jnp.bfloat16)))
    start_grads = (jnp.zeros((TOKENS, DH), jnp.float32), jnp.zeros((TOKENS, DH), jnp.float32))
    (keys_grad, values_grad), (attn_all, query_all) = lax.scan(shard_step, start_grads, jnp.arange(N_CTX, dtype=jnp.int32))
    attn_out = attn_all.reshape(TOKENS, HEADS, DH)
    grad_queries = query_all.reshape(TOKENS, HEADS, DH)
    return (attn_out, grad_queries, keys_grad.astype(jnp.bfloat16), values_grad.astype(jnp.bfloat16))
```

```python
import functools
import math

import jax
import jax.numpy as jnp
from jax import lax
from jax.experimental import pallas as pl
from jax.experimental.pallas import tpu as pltpu
from jax.sharding import PartitionSpec as P

NEG = -1e30
AXES = ("ctx", "head")
SLOTS = 4
VMEM = pl.BlockSpec(memory_space=pltpu.VMEM)
SMEM = pl.BlockSpec(memory_space=pltpu.SMEM)
PARAMS = pltpu.CompilerParams(vmem_limit_bytes=40 * 1024 * 1024)
F32 = jnp.float32
BF16 = jnp.bfloat16

TABLES = {
    128: ((64, 8), (4, 32), (16, 2), (0, 1)),
    16: ((8, 2), (4, 1), (None, None), (0, None)),
}


def call(kernel, out_shape, in_specs, flops, moved, exps):
    outs = jax.tree.map(lambda _: VMEM, out_shape)
    return pl.pallas_call(
        kernel,
        out_shape=out_shape,
        in_specs=in_specs,
        out_specs=outs,
        compiler_params=PARAMS,
        cost_estimate=pl.CostEstimate(flops=flops, bytes_accessed=moved, transcendentals=exps),
    )


def mask_kernel(meta, lengths, pattern, bias_ref):
    rows = bias_ref.shape[2]
    block = 128
    count = rows // block
    own = meta[0]
    lane = lax.broadcasted_iota(jnp.int32, (8, rows), 1)
    sub = lax.broadcasted_iota(jnp.int32, (8, rows), 0)
    base = jnp.full((8, rows), own * rows, jnp.int32)
    for slot in range(SLOTS):
        base = jnp.where(sub == slot + 1, meta[1 + slot] * rows, base)
    pos = base + lane

    def add_doc(index, carry):
        end, total = carry
        end = end + lengths[index]
        return end, total + jnp.where(pos >= end, 1.0, 0.0)

    docs = lax.fori_loop(
        0, lengths.shape[0], add_doc, (jnp.int32(0), jnp.zeros((8, rows), F32)), unroll=8
    )[1]
    query_doc = docs[0:1]
    query_pos = pos[0:1]
    down = lax.broadcasted_iota(jnp.int32, (block, rows), 0)
    for slot in range(SLOTS):
        partner = meta[1 + slot]
        valid = meta[1 + SLOTS + slot]
        for kb in range(count):
            key_doc = docs[slot + 1 : slot + 2, kb * block : (kb + 1) * block]
            key_doc = jnp.broadcast_to(key_doc, (block, block)).T
            for qb in range(count):
                cols = slice(qb * block, (qb + 1) * block)
                same = key_doc == query_doc[:, cols]
                early = down[:, cols] + (partner * rows + kb * block) <= query_pos[:, cols]
                live = jnp.where(pattern[qb, partner * count + kb] * valid == 1, 0.0, NEG)
                bias_ref[slot, kb * block : (kb + 1) * block, cols] = (
                    jnp.where(same & early, 0.0, NEG) + live
                )


def dot(a, b, dims):
    return lax.dot_general(a, b, (dims, ((), ())), preferred_element_type=F32)


NN = ((1,), (0,))
NT = ((1,), (1,))


def head_rows(own_ref, other_ref, head, rows, which):
    half = own_ref.shape[0] // 2
    ref = own_ref if head < 2 else other_ref
    start = which * half + (head % 2) * rows
    return ref[start : start + rows, :]


def forward_kernel(slots, first, last, *refs):
    own_ref, other_ref, bias_ref = refs[:3]
    kv_refs = refs[3 : 3 + len(slots)]
    rest = refs[3 + len(slots) :]
    if first:
        stat_out, out_out = rest
    else:
        stat_in, out_in, stat_out, out_out = rest
    rows = bias_ref.shape[1]
    dim = own_ref.shape[1]
    factor = math.log2(math.e) / math.sqrt(dim)
    values_t = [kv[rows:, :].T for kv in kv_refs]
    for head in range(4):
        cols = slice(head * rows, (head + 1) * rows)
        query = head_rows(own_ref, other_ref, head, rows, 0)
        if first:
            top = jnp.full((1, rows), NEG, F32)
            total = jnp.zeros((1, rows), F32)
            out = jnp.zeros((dim, rows), F32)
        else:
            top = stat_in[0:1, cols]
            total = stat_in[1:2, cols]
            out = out_in[:, cols]
        for place, slot in enumerate(slots):
            scores = dot(kv_refs[place][:rows, :], query, NT) * factor + bias_ref[slot]
            new_top = jnp.maximum(top, jnp.max(scores, axis=0, keepdims=True))
            probs = jnp.exp2(scores - new_top)
            fade = jnp.exp2(top - new_top)
            total = total * fade + jnp.sum(probs, axis=0, keepdims=True)
            out = out * fade + dot(values_t[place], probs.astype(BF16), NN)
            top = new_top
        out_out[:, cols] = out
        stat_out[0:1, cols] = top
        stat_out[1:2, cols] = total
        if last:
            grad_t = head_rows(own_ref, other_ref, head, rows, 1).T.astype(F32)
            stat_out[2:3, cols] = jnp.sum(grad_t * out, axis=0, keepdims=True)
        else:
            stat_out[2:3, cols] = jnp.zeros((1, rows), F32)
        stat_out[3:8, cols] = jnp.zeros((5, rows), F32)


def merged(stat_ref, other_stat_ref, head, rows):
    cols = slice(head * rows, (head + 1) * rows)
    other = ((head + 2) % 4) * rows
    other_cols = slice(other, other + rows)
    top_a, top_b = stat_ref[0:1, cols], other_stat_ref[0:1, other_cols]
    top = jnp.maximum(top_a, top_b)
    fade_a, fade_b = jnp.exp2(top_a - top), jnp.exp2(top_b - top)
    total = stat_ref[1:2, cols] * fade_a + other_stat_ref[1:2, other_cols] * fade_b
    inner = stat_ref[2:3, cols] * fade_a + other_stat_ref[2:3, other_cols] * fade_b
    return top + jnp.log2(total), inner / total, fade_a, fade_b, total


def backward_kernel(slot, first, last, *refs):
    own_ref, other_ref, bias_ref, kv_ref, stat_ref, other_stat_ref = refs[:6]
    rest = refs[6:]
    rows = bias_ref.shape[1]
    dim = own_ref.shape[1]
    out_ref = None
    if last:
        out_ref, rest = rest[0], rest[1:]
    query_in = None
    if not first:
        query_in, rest = rest[0], rest[1:]
    grad_kv_ref, query_out = rest[:2]
    factor = math.log2(math.e) / math.sqrt(dim)
    scale = 1.0 / math.sqrt(dim)
    key = kv_ref[:rows, :]
    value = kv_ref[rows:, :]
    key_t = key.T
    grad_key = jnp.zeros((rows, dim), F32)
    grad_value = jnp.zeros((rows, dim), F32)
    for head in range(4):
        cols = slice(head * rows, (head + 1) * rows)
        query = head_rows(own_ref, other_ref, head, rows, 0)
        grad = head_rows(own_ref, other_ref, head, rows, 1)
        norm, inner, _, _, _ = merged(stat_ref, other_stat_ref, head, rows)
        scores = dot(key, query, NT) * factor + bias_ref[slot]
        probs = jnp.exp2(scores - norm)
        grad_value = grad_value + dot(probs.astype(BF16), grad, NN)
        grad_score = (probs * (dot(value, grad, NT) - inner)).astype(BF16)
        grad_key = grad_key + dot(grad_score, query, NN)
        part = dot(key_t, grad_score, NN) * scale
        if not first:
            part = query_in[:, cols] + part
        query_out[:, cols] = part
        if last and head >= 2:
            send_ref = rest[2]
            there = slice((head - 2) * rows, (head - 1) * rows)
            send_ref[:dim, there] = (out_ref[:, cols] / stat_ref[1:2, cols]).astype(BF16)
            send_ref[dim:, there] = part.astype(BF16)
    grad_kv_ref[:rows, :] = (grad_key * scale).astype(BF16)
    grad_kv_ref[rows:, :] = grad_value.astype(BF16)


def finish_kernel(stat_ref, other_stat_ref, out_ref, query_ref, got_ref, attn_ref, grad_ref):
    rows = attn_ref.shape[0] // 2
    dim = attn_ref.shape[1]
    for head in range(2):
        cols = slice(head * rows, (head + 1) * rows)
        _, _, fade_a, fade_b, total = merged(stat_ref, other_stat_ref, head, rows)
        other = slice((head + 2) * rows, (head + 3) * rows)
        weight_b = fade_b * other_stat_ref[1:2, other] / total
        out = out_ref[:, cols] * (fade_a / total) + got_ref[:dim, cols].astype(F32) * weight_b
        attn_ref[cols, :] = out.T.astype(BF16)
        grad = query_ref[:, cols] + got_ref[dim:, cols].astype(F32)
        grad_ref[cols, :] = grad.T.astype(BF16)


def local(queries, key_rows, value_rows, grad_out, doc_lengths, block_pattern):
    rows, heads, dim = queries.shape
    width = lax.axis_size("ctx")
    lanes = lax.axis_size("head")
    table = TABLES[width]
    edge = width * 3 // 4
    own = lax.axis_index("ctx")
    lane = lax.axis_index("head") % 2

    def lane_pairs(shifts, back):
        pairs = []
        for which, shift in enumerate(shifts):
            if not shift:
                continue
            for source in range(width - shift):
                target = source + shift
                if (source < edge) != (target < edge):
                    continue
                for place in range(which, lanes, 2):
                    pair = (source * lanes + place, target * lanes + place)
                    pairs.append(pair[::-1] if back else pair)
        return pairs

    def swap_pairs(partner):
        return [
            (group * lanes + place, group * lanes + partner(place))
            for group in range(width)
            for place in range(lanes)
        ]

    near = swap_pairs(lambda place: place ^ 1)
    far = swap_pairs(lambda place: lanes - 1 - place)

    own_kv = jnp.concatenate([key_rows, value_rows], axis=0)
    sent = [bool([s for s in shifts if s]) for shifts in table]
    held = []
    held.append(lax.ppermute(own_kv, AXES, lane_pairs(table[0], False)))
    own_qg = jnp.concatenate(
        [
            queries.transpose(1, 0, 2).reshape(heads * rows, dim),
            grad_out.transpose(1, 0, 2).reshape(heads * rows, dim),
        ],
        axis=0,
    )
    other_qg = lax.ppermute(own_qg, AXES, near)
    for slot in range(1, SLOTS):
        if sent[slot]:
            got = lax.ppermute(own_kv, AXES, lane_pairs(table[slot], False))
        else:
            got = own_kv
        if table[slot][0] == 0:
            got = jnp.where(lane == 0, own_kv, got)
        held.append(got)

    shift = jnp.array([[0 if s is None else s for s in pair] for pair in table], jnp.int32)
    exists = jnp.array([[0 if s is None else 1 for s in pair] for pair in table], jnp.int32)
    partner = own - shift[:, lane]
    valid = exists[:, lane] * (partner >= 0)
    meta = jnp.concatenate(
        [jnp.reshape(own, (1,)), jnp.maximum(partner, 0), valid.astype(jnp.int32)]
    ).astype(jnp.int32)
    bias = call(
        mask_kernel,
        jax.ShapeDtypeStruct((SLOTS, rows, rows), F32),
        [SMEM, SMEM, SMEM],
        0,
        SLOTS * rows * rows * 4,
        0,
    )(meta, doc_lengths, block_pattern)

    columns = 4 * rows
    stat_shape = jax.ShapeDtypeStruct((8, columns), F32)
    wide_shape = jax.ShapeDtypeStruct((dim, columns), F32)
    unit = 2 * rows * columns * dim

    def forward(slots, carry, last):
        first = carry is None
        kernel = functools.partial(forward_kernel, slots, first, last)
        args = [own_qg, other_qg, bias] + [held[s] for s in slots] + list(carry or ())
        return call(
            kernel,
            (stat_shape, wide_shape),
            [VMEM] * len(args),
            2 * unit * len(slots),
            4 << 20,
            rows * columns * len(slots),
        )(*args)

    stat, out = forward((0, 1), None, False)
    stat, out = forward((2, 3), (stat, out), True)
    other_stat = lax.ppermute(stat, AXES, near)

    kv_shape = jax.ShapeDtypeStruct((2 * rows, dim), BF16)
    send_shape = jax.ShapeDtypeStruct((2 * dim, 2 * rows), BF16)
    returned = []
    query_grad = None
    for slot in range(SLOTS):
        first, last = slot == 0, slot == SLOTS - 1
        kernel = functools.partial(backward_kernel, slot, first, last)
        args = [own_qg, other_qg, bias, held[slot], stat, other_stat]
        if last:
            args.append(out)
        if not first:
            args.append(query_grad)
        shapes = (kv_shape, wide_shape) + ((send_shape,) if last else ())
        results = call(
            kernel, shapes, [VMEM] * len(args), 5 * unit, 4 << 20, rows * columns
        )(*args)
        grad_kv, query_grad = results[:2]
        if sent[slot]:
            back = lax.ppermute(grad_kv, AXES, lane_pairs(table[slot], True))
        else:
            back = jnp.zeros_like(grad_kv)
        if table[slot][0] == 0:
            back = jnp.where(lane == 0, grad_kv, back)
        returned.append(back)
    got = lax.ppermute(results[2], AXES, near)
    total = sum(back.astype(F32) for back in returned).astype(BF16)
    total = (total.astype(F32) + lax.ppermute(total, AXES, near).astype(F32)).astype(BF16)
    total = (total.astype(F32) + lax.ppermute(total, AXES, far).astype(F32)).astype(BF16)

    flat = jax.ShapeDtypeStruct((heads * rows, dim), BF16)
    attn, grad_q = call(
        finish_kernel, (flat, flat), [VMEM] * 5, 0, 2 << 20, 0
    )(stat, other_stat, out, query_grad, got)

    def by_token(array):
        return array.reshape(heads, rows, dim).transpose(1, 0, 2)

    return by_token(attn), by_token(grad_q), total[:rows], total[rows:]


def solution(mesh):
    wide, flat = P("ctx", "head", None), P("ctx", None)
    return jax.shard_map(
        local,
        mesh=mesh,
        in_specs=(wide, flat, flat, wide, P(), flat),
        out_specs=(wide, wide, flat, flat),
        check_vma=False,
    )
```

```python
import functools
import math

import jax
import jax.numpy as jnp
from jax import lax
from jax.experimental import pallas as pl
from jax.experimental.pallas import tpu as pltpu
from jax.sharding import PartitionSpec as P

NEG = -1e30
AXES = ("ctx", "head")
SLOTS = 4
VMEM = pl.BlockSpec(memory_space=pltpu.VMEM)
HBM = pl.BlockSpec(memory_space=pltpu.HBM)
PARAMS = pltpu.CompilerParams(vmem_limit_bytes=40 * 1024 * 1024)
F32 = jnp.float32
BF16 = jnp.bfloat16

TABLES = {
    128: ((64, 8), (4, 32), (16, 2), (1, 0)),
    16: ((8, 2), (4, 1), (None, None), (None, 0)),
}


def call(kernel, out_shape, in_specs, flops, moved, exps):
    outs = jax.tree.map(lambda _: VMEM, out_shape)
    return pl.pallas_call(
        kernel,
        out_shape=out_shape,
        in_specs=in_specs,
        out_specs=outs,
        compiler_params=PARAMS,
        cost_estimate=pl.CostEstimate(flops=flops, bytes_accessed=moved, transcendentals=exps),
    )


def pack_kernel(key_ref, value_ref, query_ref, grad_ref, kv_ref, qg_ref, sems):
    rows, wide = key_ref.shape[0], query_ref.shape[0]
    copies = [
        pltpu.make_async_copy(key_ref, kv_ref.at[pl.ds(0, rows)], sems.at[0]),
        pltpu.make_async_copy(value_ref, kv_ref.at[pl.ds(rows, rows)], sems.at[1]),
        pltpu.make_async_copy(query_ref, qg_ref.at[pl.ds(0, wide)], sems.at[2]),
        pltpu.make_async_copy(grad_ref, qg_ref.at[pl.ds(wide, wide)], sems.at[3]),
    ]
    for copy in copies:
        copy.start()
    for copy in copies:
        copy.wait()


def mask_kernel(table, lengths_ref, pattern_ref, bias_ref, lengths, pattern, sems):
    copies = [
        pltpu.make_async_copy(lengths_ref, lengths, sems.at[0]),
        pltpu.make_async_copy(pattern_ref, pattern, sems.at[1]),
    ]
    for copy in copies:
        copy.start()
    rows, wide = bias_ref.shape[1:]
    block = 128
    count = rows // block
    span = wide // count
    own = lax.axis_index("ctx")
    lane = lax.rem(lax.axis_index("head"), 2)
    valid, partners = [], []
    for pair in table:
        shift = jnp.where(lane == 0, pair[0] or 0, pair[1] or 0)
        exists = jnp.where(lane == 0, int(pair[0] is not None), int(pair[1] is not None))
        valid.append(jnp.where(own >= shift, exists, 0))
        partners.append(jnp.maximum(own - shift, 0))
    column = lax.broadcasted_iota(jnp.int32, (8, wide), 1)
    sub = lax.broadcasted_iota(jnp.int32, (8, wide), 0)
    pos = own * rows + lax.shift_right_logical(column, 1)
    for slot in range(SLOTS):
        pos = jnp.where(sub == slot + 1, partners[slot] * rows + column, pos)
    for copy in copies:
        copy.wait()

    def add_doc(index, carry):
        end, total = carry
        end = end + lengths[index]
        return end, total + jnp.where(pos >= end, 1.0, 0.0)

    docs = lax.fori_loop(
        0, lengths.shape[0], add_doc, (jnp.int32(0), jnp.zeros((8, wide), F32)), unroll=8
    )[1]
    query_doc = docs[0:1]
    query_pos = pos[0:1]
    down = lax.broadcasted_iota(jnp.int32, (block, span), 0)
    for slot in range(SLOTS):
        for kb in range(count):
            key_doc = docs[slot + 1 : slot + 2, kb * block : (kb + 1) * block]
            key_doc = jnp.broadcast_to(key_doc, (block, block)).T
            key_doc = jnp.concatenate([key_doc] * (span // block), axis=1)
            for qb in range(count):
                cols = slice(qb * span, (qb + 1) * span)
                same = key_doc == query_doc[:, cols]
                early = down + (partners[slot] * rows + kb * block) <= query_pos[:, cols]
                alive = pattern[qb, partners[slot] * count + kb] * valid[slot]
                live = jnp.where(alive == 1, 0.0, NEG)
                bias_ref[slot, kb * block : (kb + 1) * block, cols] = (
                    jnp.where(same & early, 0.0, NEG) + live
                )


def dot(a, b, dims):
    return lax.dot_general(a, b, (dims, ((), ())), preferred_element_type=F32)


NN = ((1,), (0,))
NT = ((1,), (1,))


def part_rows(ref, which):
    half = ref.shape[0] // 2
    return ref[which * half : (which + 1) * half, :]


def columns_of(ref, part):
    half = ref.shape[1] // 2
    return slice(part * half, (part + 1) * half)


def forward_kernel(slots, first, last, *refs):
    sides = refs[:2]
    bias_ref = refs[2]
    kv_refs = refs[3 : 3 + len(slots)]
    rest = refs[3 + len(slots) :]
    if first:
        stat_out, out_out = rest
    else:
        stat_in, out_in, stat_out, out_out = rest
    rows, wide = bias_ref.shape[1:]
    factor = math.log2(math.e) / math.sqrt(kv_refs[0].shape[1])
    values_t = [kv[rows:, :].T for kv in kv_refs]
    for part, side in enumerate(sides):
        cols = columns_of(stat_out, part)
        query = part_rows(side, 0)
        scores = [
            dot(kv[:rows, :], query, NT) * factor + bias_ref[slot]
            for kv, slot in zip(kv_refs, slots)
        ]
        top = functools.reduce(
            jnp.maximum, [jnp.max(piece, axis=0, keepdims=True) for piece in scores]
        )
        if not first:
            top = jnp.maximum(top, stat_in[0:1, cols])
        probs = [jnp.exp2(piece - top) for piece in scores]
        total = sum(jnp.sum(piece, axis=0, keepdims=True) for piece in probs)
        out = sum(dot(value, piece.astype(BF16), NN) for value, piece in zip(values_t, probs))
        if not first:
            fade = jnp.exp2(stat_in[0:1, cols] - top)
            total = total + stat_in[1:2, cols] * fade
            out = out + out_in[:, cols] * fade
        out_out[:, cols] = out
        stat_out[0:1, cols] = top
        stat_out[1:2, cols] = total
        if last:
            grad_t = part_rows(side, 1).T.astype(F32)
            stat_out[2:3, cols] = jnp.sum(grad_t * out, axis=0, keepdims=True)
            stat_out[3:4, cols] = jnp.zeros((1, wide), F32)
        else:
            stat_out[2:4, cols] = jnp.zeros((2, wide), F32)


def merged(stat_ref, other_stat_ref, part):
    cols = columns_of(stat_ref, part)
    other = columns_of(stat_ref, 1 - part)
    top_a, top_b = stat_ref[0:1, cols], other_stat_ref[0:1, other]
    top = jnp.maximum(top_a, top_b)
    fade_a, fade_b = jnp.exp2(top_a - top), jnp.exp2(top_b - top)
    total_b = other_stat_ref[1:2, other] * fade_b
    total = stat_ref[1:2, cols] * fade_a + total_b
    inner = stat_ref[2:3, cols] * fade_a + other_stat_ref[2:3, other] * fade_b
    return top + jnp.log2(total), inner / total, fade_a / total, total_b / total


def backward_kernel(slot, first, last, *refs):
    sides = refs[:2]
    bias_ref, kv_ref, stat_ref, other_stat_ref = refs[2:6]
    rest = refs[6:]
    rows = bias_ref.shape[1]
    dim = kv_ref.shape[1]
    if last:
        out_ref, rest = rest[0], rest[1:]
    if not first:
        query_in, rest = rest[0], rest[1:]
    grad_kv_ref, query_out = rest[:2]
    factor = math.log2(math.e) / math.sqrt(dim)
    scale = 1.0 / math.sqrt(dim)
    key = kv_ref[:rows, :]
    value = kv_ref[rows:, :]
    key_t = key.T
    grad_key = jnp.zeros((rows, dim), F32)
    grad_value = jnp.zeros((rows, dim), F32)
    for part, side in enumerate(sides):
        cols = columns_of(stat_ref, part)
        query, grad = part_rows(side, 0), part_rows(side, 1)
        norm, inner, _, _ = merged(stat_ref, other_stat_ref, part)
        scores = dot(key, query, NT) * factor + bias_ref[slot]
        probs = jnp.exp2(scores - norm)
        grad_value = grad_value + dot(probs.astype(BF16), grad, NN)
        grad_score = (probs * (dot(value, grad, NT) - inner)).astype(BF16)
        grad_key = grad_key + dot(grad_score, query, NN)
        grad_query = dot(key_t, grad_score, NN) * scale
        if not first:
            grad_query = query_in[:, cols] + grad_query
        query_out[:, cols] = grad_query
        if last and part == 1:
            send_ref = rest[2]
            send_ref[:dim, :] = (out_ref[:, cols] / stat_ref[1:2, cols]).astype(BF16)
            send_ref[dim:, :] = grad_query.astype(BF16)
    grad_kv_ref[:rows, :] = (grad_key * scale).astype(BF16)
    grad_kv_ref[rows:, :] = grad_value.astype(BF16)


def finish_kernel(stat_ref, other_stat_ref, out_ref, query_ref, got_ref, attn_ref, grad_ref):
    dim = attn_ref.shape[1]
    cols = columns_of(stat_ref, 0)
    _, _, weight_a, weight_b = merged(stat_ref, other_stat_ref, 0)
    out = out_ref[:, cols] * weight_a + got_ref[:dim, :].astype(F32) * weight_b
    attn_ref[...] = out.T.astype(BF16)
    grad = query_ref[:, cols] + got_ref[dim:, :].astype(F32)
    grad_ref[...] = grad.T.astype(BF16)


def sum_kernel(count, *refs):
    total = sum(ref[...].astype(F32) for ref in refs[:count]).astype(BF16)
    start = 0
    for ref in refs[count:]:
        ref[...] = total[start : start + ref.shape[0], :]
        start += ref.shape[0]


def local(queries, key_rows, value_rows, grad_out, doc_lengths, block_pattern):
    rows, heads, dim = queries.shape
    width = lax.axis_size("ctx")
    lanes = lax.axis_size("head")
    table = TABLES[width]
    edge = width * 3 // 4

    def lane_pairs(shifts, back):
        pairs = []
        for which, shift in enumerate(shifts):
            if shift is None:
                continue
            for source in range(width - shift):
                target = source + shift
                if (source < edge) != (target < edge):
                    continue
                for place in range(which, lanes, 2):
                    pair = (source * lanes + place, target * lanes + place)
                    pairs.append(pair[::-1] if back else pair)
        return pairs

    def swap_pairs(partner):
        return [
            (group * lanes + place, group * lanes + partner(place))
            for group in range(width)
            for place in range(lanes)
        ]

    def send(value, pairs):
        return lax.ppermute(value, AXES, pairs)

    near = swap_pairs(lambda place: place ^ 1)
    far = swap_pairs(lambda place: lanes - 1 - place)

    kv_shape = jax.ShapeDtypeStruct((2 * rows, dim), BF16)
    qg_shape = jax.ShapeDtypeStruct((2 * heads * rows, dim), BF16)
    own_kv, own_qg = pl.pallas_call(
        pack_kernel,
        out_shape=(kv_shape, qg_shape),
        in_specs=[HBM] * 4,
        out_specs=(VMEM, VMEM),
        scratch_shapes=[pltpu.SemaphoreType.DMA((4,))],
        compiler_params=PARAMS,
    )(
        key_rows,
        value_rows,
        queries.reshape(rows * heads, dim),
        grad_out.reshape(rows * heads, dim),
    )
    held = [send(own_kv, lane_pairs(table[0], False))]
    other_qg = send(own_qg, near)
    for slot in range(1, SLOTS):
        held.append(send(own_kv, lane_pairs(table[slot], False)))

    bias = pl.pallas_call(
        functools.partial(mask_kernel, table),
        out_shape=jax.ShapeDtypeStruct((SLOTS, rows, heads * rows), F32),
        in_specs=[HBM, HBM],
        out_specs=VMEM,
        scratch_shapes=[
            pltpu.SMEM(doc_lengths.shape, jnp.int32),
            pltpu.SMEM(block_pattern.shape, jnp.int32),
            pltpu.SemaphoreType.DMA((2,)),
        ],
        compiler_params=PARAMS,
    )(doc_lengths, block_pattern)

    columns = 2 * heads * rows
    stat_shape = jax.ShapeDtypeStruct((4, columns), F32)
    wide_shape = jax.ShapeDtypeStruct((dim, columns), F32)
    unit = 2 * rows * columns * dim

    def forward(slots, carry, last):
        first = carry is None
        kernel = functools.partial(forward_kernel, slots, first, last)
        args = [own_qg, other_qg, bias] + [held[s] for s in slots] + list(carry or ())
        return call(
            kernel,
            (stat_shape, wide_shape),
            [VMEM] * len(args),
            2 * unit * len(slots),
            4 << 20,
            rows * columns * len(slots),
        )(*args)

    stat, out = forward((0, 1), None, False)
    stat, out = forward((2, 3), (stat, out), True)
    other_stat = send(stat, near)

    send_shape = jax.ShapeDtypeStruct((2 * dim, heads * rows), BF16)
    returned = []
    query_grad = None
    for slot in range(SLOTS):
        first, last = slot == 0, slot == SLOTS - 1
        kernel = functools.partial(backward_kernel, slot, first, last)
        args = [own_qg, other_qg, bias, held[slot], stat, other_stat]
        if last:
            args.append(out)
        if not first:
            args.append(query_grad)
        shapes = (kv_shape, wide_shape) + ((send_shape,) if last else ())
        results = call(
            kernel, shapes, [VMEM] * len(args), 5 * unit, 4 << 20, rows * columns
        )(*args)
        grad_kv, query_grad = results[:2]
        returned.append(send(grad_kv, lane_pairs(table[slot], True)))
    got = send(results[2], near)

    def add(pieces, shapes):
        kernel = functools.partial(sum_kernel, len(pieces))
        return call(kernel, shapes, [VMEM] * len(pieces), 0, 1 << 20, 0)(*pieces)

    total = add(returned, (kv_shape,))[0]
    total = add((total, send(total, near)), (kv_shape,))[0]
    key_shape = jax.ShapeDtypeStruct((rows, dim), BF16)
    grad_keys, grad_values = add((total, send(total, far)), (key_shape, key_shape))

    flat = jax.ShapeDtypeStruct((heads * rows, dim), BF16)
    attn, grad_q = call(finish_kernel, (flat, flat), [VMEM] * 5, 0, 2 << 20, 0)(
        stat, other_stat, out, query_grad, got
    )
    shape = (rows, heads, dim)
    return attn.reshape(shape), grad_q.reshape(shape), grad_keys, grad_values


def solution(mesh):
    wide, flat = P("ctx", "head", None), P("ctx", None)

    return jax.shard_map(
        local,
        mesh=mesh,
        in_specs=(wide, flat, flat, wide, P(), flat),
        out_specs=(wide, wide, flat, flat),
        check_vma=False,
    )
```

```python
import functools
import math

import jax
import jax.numpy as jnp
from jax import lax
from jax.experimental import pallas as pl
from jax.experimental.pallas import tpu as pltpu
from jax.sharding import PartitionSpec as P

NEG = -1e30
AXES = ("ctx", "head")
SLOTS = 4
VMEM = pl.BlockSpec(memory_space=pltpu.VMEM)
HBM = pl.BlockSpec(memory_space=pltpu.HBM)
PARAMS = pltpu.CompilerParams(vmem_limit_bytes=40 * 1024 * 1024)
F32 = jnp.float32
BF16 = jnp.bfloat16

TABLES = {
    128: ((64, 8), (4, 32), (16, 2), (1, 0)),
    16: ((8, 2), (4, 1), (None, None), (None, 0)),
}


def call(kernel, out_shape, in_specs, flops, moved, exps):
    outs = jax.tree.map(lambda _: VMEM, out_shape)
    return pl.pallas_call(
        kernel,
        out_shape=out_shape,
        in_specs=in_specs,
        out_specs=outs,
        compiler_params=PARAMS,
        cost_estimate=pl.CostEstimate(flops=flops, bytes_accessed=moved, transcendentals=exps),
    )


def pack_kernel(key_ref, value_ref, query_ref, grad_ref, kv_ref, qg_ref, sems):
    rows, wide = key_ref.shape[0], query_ref.shape[0]
    copies = [
        pltpu.make_async_copy(key_ref, kv_ref.at[pl.ds(0, rows)], sems.at[0]),
        pltpu.make_async_copy(value_ref, kv_ref.at[pl.ds(rows, rows)], sems.at[1]),
        pltpu.make_async_copy(query_ref, qg_ref.at[pl.ds(0, wide)], sems.at[2]),
        pltpu.make_async_copy(grad_ref, qg_ref.at[pl.ds(wide, wide)], sems.at[3]),
    ]
    for copy in copies:
        copy.start()
    for copy in copies:
        copy.wait()


def mask_kernel(table, lengths_ref, pattern_ref, bias_ref, lengths, pattern, sems):
    copies = [
        pltpu.make_async_copy(lengths_ref, lengths, sems.at[0]),
        pltpu.make_async_copy(pattern_ref, pattern, sems.at[1]),
    ]
    for copy in copies:
        copy.start()
    rows, wide = bias_ref.shape[1:]
    block = 128
    count = rows // block
    span = wide // count
    own = lax.axis_index("ctx")
    lane = lax.rem(lax.axis_index("head"), 2)
    valid, partners = [], []
    for pair in table:
        shift = jnp.where(lane == 0, pair[0] or 0, pair[1] or 0)
        exists = jnp.where(lane == 0, int(pair[0] is not None), int(pair[1] is not None))
        valid.append(jnp.where(own >= shift, exists, 0))
        partners.append(jnp.maximum(own - shift, 0))
    column = lax.broadcasted_iota(jnp.int32, (8, wide), 1)
    sub = lax.broadcasted_iota(jnp.int32, (8, wide), 0)
    pos = own * rows + lax.shift_right_logical(column, 1)
    for slot in range(SLOTS):
        pos = jnp.where(sub == slot + 1, partners[slot] * rows + column, pos)
    for copy in copies:
        copy.wait()

    def add_doc(index, carry):
        end, total = carry
        end = end + lengths[index]
        return end, total + jnp.where(pos >= end, 1.0, 0.0)

    docs = lax.fori_loop(
        0, lengths.shape[0], add_doc, (jnp.int32(0), jnp.zeros((8, wide), F32)), unroll=8
    )[1]
    query_doc = docs[0:1]
    query_pos = pos[0:1]
    down = lax.broadcasted_iota(jnp.int32, (block, span), 0)
    for slot, pair in enumerate(table):
        for kb in range(count):
            key_doc = docs[slot + 1 : slot + 2, kb * block : (kb + 1) * block]
            key_doc = jnp.broadcast_to(key_doc, (block, block)).T
            key_doc = jnp.concatenate([key_doc] * (span // block), axis=1)
            for qb in range(count):
                cols = slice(qb * span, (qb + 1) * span)
                open_pair = key_doc == query_doc[:, cols]
                if 0 in pair:
                    early = down + (partners[slot] * rows + kb * block) <= query_pos[:, cols]
                    open_pair = open_pair & early
                alive = pattern[qb, partners[slot] * count + kb] * valid[slot]
                live = jnp.where(alive == 1, 0.0, NEG)
                bias_ref[slot, kb * block : (kb + 1) * block, cols] = jnp.where(
                    open_pair, live, NEG
                )


def dot(a, b, dims):
    return lax.dot_general(a, b, (dims, ((), ())), preferred_element_type=F32)


NN = ((1,), (0,))
NT = ((1,), (1,))


def part_rows(ref, which):
    half = ref.shape[0] // 2
    return ref[which * half : (which + 1) * half, :]


def columns_of(ref, part):
    half = ref.shape[1] // 2
    return slice(part * half, (part + 1) * half)


def forward_kernel(slots, first, last, *refs):
    sides = refs[:2]
    bias_ref = refs[2]
    kv_refs = refs[3 : 3 + len(slots)]
    rest = refs[3 + len(slots) :]
    if not first:
        stat_in, out_in, *rest = rest
    stat_out, out_out = rest[:2]
    rows, wide = bias_ref.shape[1:]
    factor = math.log2(math.e) / math.sqrt(kv_refs[0].shape[1])
    values_t = [kv[rows:, :].T for kv in kv_refs]
    for part, side in enumerate(sides):
        cols = columns_of(stat_out, part)
        query = part_rows(side, 0)
        scores = [
            dot(kv[:rows, :], query, NT) * factor + bias_ref[slot]
            for kv, slot in zip(kv_refs, slots)
        ]
        top = functools.reduce(
            jnp.maximum, [jnp.max(piece, axis=0, keepdims=True) for piece in scores]
        )
        if not first:
            top = jnp.maximum(top, stat_in[0:1, cols])
        probs = [jnp.exp2(piece - top) for piece in scores]
        total = sum(jnp.sum(piece, axis=0, keepdims=True) for piece in probs)
        out = sum(dot(value, piece.astype(BF16), NN) for value, piece in zip(values_t, probs))
        if not first:
            fade = jnp.exp2(stat_in[0:1, cols] - top)
            total = total + stat_in[1:2, cols] * fade
            out = out + out_in[:, cols] * fade
        out_out[:, cols] = out
        stat_out[0:1, cols] = top
        stat_out[1:2, cols] = total
        if last:
            grad_t = part_rows(side, 1).T.astype(F32)
            stat_out[2:3, cols] = jnp.sum(grad_t * out, axis=0, keepdims=True)
            stat_out[3:4, cols] = jnp.zeros((1, wide), F32)
            if part == 1:
                rest[2][...] = (out / total).astype(BF16)
        else:
            stat_out[2:4, cols] = jnp.zeros((2, wide), F32)


def merged(stat_ref, other_stat_ref, part):
    cols = columns_of(stat_ref, part)
    other = columns_of(stat_ref, 1 - part)
    top_a, top_b = stat_ref[0:1, cols], other_stat_ref[0:1, other]
    top = jnp.maximum(top_a, top_b)
    fade_a, fade_b = jnp.exp2(top_a - top), jnp.exp2(top_b - top)
    total_b = other_stat_ref[1:2, other] * fade_b
    total = stat_ref[1:2, cols] * fade_a + total_b
    inner = stat_ref[2:3, cols] * fade_a + other_stat_ref[2:3, other] * fade_b
    return top + jnp.log2(total), inner / total, fade_a / total, total_b / total


def backward_kernel(slot, first, last, *refs):
    sides = refs[:2]
    bias_ref, kv_ref, stat_ref, other_stat_ref = refs[2:6]
    rest = refs[6:]
    rows = bias_ref.shape[1]
    dim = kv_ref.shape[1]
    if not first:
        query_in, rest = rest[0], rest[1:]
    grad_kv_ref, query_out = rest[:2]
    factor = math.log2(math.e) / math.sqrt(dim)
    scale = 1.0 / math.sqrt(dim)
    key = kv_ref[:rows, :]
    value = kv_ref[rows:, :]
    key_t = key.T
    grad_key = jnp.zeros((rows, dim), F32)
    grad_value = jnp.zeros((rows, dim), F32)
    for part, side in enumerate(sides):
        cols = columns_of(stat_ref, part)
        query, grad = part_rows(side, 0), part_rows(side, 1)
        norm, inner, _, _ = merged(stat_ref, other_stat_ref, part)
        scores = dot(key, query, NT) * factor + bias_ref[slot]
        probs = jnp.exp2(scores - norm)
        grad_value = grad_value + dot(probs.astype(BF16), grad, NN)
        grad_score = (probs * (dot(value, grad, NT) - inner)).astype(BF16)
        grad_key = grad_key + dot(grad_score, query, NN)
        grad_query = dot(key_t, grad_score, NN) * scale
        if not first:
            grad_query = query_in[:, cols] + grad_query
        query_out[:, cols] = grad_query
        if last and part == 1:
            rest[2][...] = grad_query.astype(BF16)
    grad_kv_ref[:rows, :] = (grad_key * scale).astype(BF16)
    grad_kv_ref[rows:, :] = grad_value.astype(BF16)


def finish_out_kernel(stat_ref, other_stat_ref, out_ref, got_ref, attn_ref):
    cols = columns_of(stat_ref, 0)
    _, _, weight_a, weight_b = merged(stat_ref, other_stat_ref, 0)
    out = out_ref[:, cols] * weight_a + got_ref[...].astype(F32) * weight_b
    attn_ref[...] = out.T.astype(BF16)


def finish_query_kernel(query_ref, got_ref, grad_ref):
    grad = query_ref[:, columns_of(query_ref, 0)] + got_ref[...].astype(F32)
    grad_ref[...] = grad.T.astype(BF16)


def sum_kernel(count, *refs):
    total = sum(ref[...].astype(F32) for ref in refs[:count]).astype(BF16)
    start = 0
    for ref in refs[count:]:
        ref[...] = total[start : start + ref.shape[0], :]
        start += ref.shape[0]


def local(queries, key_rows, value_rows, grad_out, doc_lengths, block_pattern):
    rows, heads, dim = queries.shape
    width = lax.axis_size("ctx")
    lanes = lax.axis_size("head")
    table = TABLES[width]
    edge = width * 3 // 4

    def lane_pairs(shifts, back):
        pairs = []
        for which, shift in enumerate(shifts):
            if shift is None:
                continue
            for source in range(width - shift):
                target = source + shift
                if (source < edge) != (target < edge):
                    continue
                for place in range(which, lanes, 2):
                    pair = (source * lanes + place, target * lanes + place)
                    pairs.append(pair[::-1] if back else pair)
        return pairs

    def swap_pairs(partner):
        return [
            (group * lanes + place, group * lanes + partner(place))
            for group in range(width)
            for place in range(lanes)
        ]

    def send(value, pairs):
        return lax.ppermute(value, AXES, pairs)

    near = swap_pairs(lambda place: place ^ 1)
    far = swap_pairs(lambda place: lanes - 1 - place)

    kv_shape = jax.ShapeDtypeStruct((2 * rows, dim), BF16)
    qg_shape = jax.ShapeDtypeStruct((2 * heads * rows, dim), BF16)
    own_kv, own_qg = pl.pallas_call(
        pack_kernel,
        out_shape=(kv_shape, qg_shape),
        in_specs=[HBM] * 4,
        out_specs=(VMEM, VMEM),
        scratch_shapes=[pltpu.SemaphoreType.DMA((4,))],
        compiler_params=pltpu.CompilerParams(vmem_limit_bytes=67043328),
    )(
        key_rows,
        value_rows,
        queries.reshape(rows * heads, dim),
        grad_out.reshape(rows * heads, dim),
    )
    held = [send(own_kv, lane_pairs(table[0], False))]
    other_qg = send(own_qg, near)
    for slot in range(1, SLOTS):
        held.append(send(own_kv, lane_pairs(table[slot], False)))

    bias = pl.pallas_call(
        functools.partial(mask_kernel, table),
        out_shape=jax.ShapeDtypeStruct((SLOTS, rows, heads * rows), F32),
        in_specs=[HBM, HBM],
        out_specs=VMEM,
        scratch_shapes=[
            pltpu.SMEM(doc_lengths.shape, jnp.int32),
            pltpu.SMEM(block_pattern.shape, jnp.int32),
            pltpu.SemaphoreType.DMA((2,)),
        ],
        compiler_params=PARAMS,
    )(doc_lengths, block_pattern)

    columns = 2 * heads * rows
    stat_shape = jax.ShapeDtypeStruct((4, columns), F32)
    wide_shape = jax.ShapeDtypeStruct((dim, columns), F32)
    unit = 2 * rows * columns * dim

    send_shape = jax.ShapeDtypeStruct((dim, heads * rows), BF16)

    def forward(slots, carry, last):
        first = carry is None
        kernel = functools.partial(forward_kernel, slots, first, last)
        args = [own_qg, other_qg, bias] + [held[s] for s in slots] + list(carry or ())
        return call(
            kernel,
            (stat_shape, wide_shape) + ((send_shape,) if last else ()),
            [VMEM] * len(args),
            2 * unit * len(slots),
            4 << 20,
            rows * columns * len(slots),
        )(*args)

    stat, out = forward((0, 1), None, False)
    stat, out, other_out = forward((2, 3), (stat, out), True)
    other_stat = send(stat, near)
    got_out = send(other_out, near)

    returned = []
    query_grad = None
    for slot in range(SLOTS):
        first, last = slot == 0, slot == SLOTS - 1
        kernel = functools.partial(backward_kernel, slot, first, last)
        args = [own_qg, other_qg, bias, held[slot], stat, other_stat]
        if not first:
            args.append(query_grad)
        shapes = (kv_shape, wide_shape) + ((send_shape,) if last else ())
        results = call(
            kernel, shapes, [VMEM] * len(args), 5 * unit, 4 << 20, rows * columns
        )(*args)
        grad_kv, query_grad = results[:2]
        returned.append(send(grad_kv, lane_pairs(table[slot], True)))
    got_query = send(results[2], near)

    def add(pieces, shapes):
        kernel = functools.partial(sum_kernel, len(pieces))
        return call(kernel, shapes, [VMEM] * len(pieces), 0, 1 << 20, 0)(*pieces)

    total = add(returned, (kv_shape,))[0]
    total = add((total, send(total, near)), (kv_shape,))[0]
    key_shape = jax.ShapeDtypeStruct((rows, dim), BF16)
    grad_keys, grad_values = add((total, send(total, far)), (key_shape, key_shape))

    flat = jax.ShapeDtypeStruct((heads * rows, dim), BF16)
    attn = call(finish_out_kernel, flat, [VMEM] * 4, 0, 1 << 20, 0)(
        stat, other_stat, out, got_out
    )
    grad_q = call(finish_query_kernel, flat, [VMEM] * 2, 0, 1 << 20, 0)(
        query_grad, got_query
    )
    shape = (rows, heads, dim)
    return attn.reshape(shape), grad_q.reshape(shape), grad_keys, grad_values


def solution(mesh):
    wide, flat = P("ctx", "head", None), P("ctx", None)

    return jax.shard_map(
        local,
        mesh=mesh,
        in_specs=(wide, flat, flat, wide, P(), flat),
        out_specs=(wide, wide, flat, flat),
        check_vma=False,
    )
```

```python
import functools
import math

import jax
import jax.numpy as jnp
from jax import lax
from jax.experimental import pallas as pl
from jax.experimental.pallas import tpu as pltpu
from jax.sharding import PartitionSpec as P

NEG = -1e30
AXES = ("ctx", "head")
SLOTS = 4
VMEM = pl.BlockSpec(memory_space=pltpu.VMEM)
HBM = pl.BlockSpec(memory_space=pltpu.HBM)
PARAMS = pltpu.CompilerParams(vmem_limit_bytes=40 * 1024 * 1024)
F32 = jnp.float32
BF16 = jnp.bfloat16

TABLES = {
    128: ((64, 32), (8, 4), (16, 2), (1, 0)),
    16: ((8, 2), (4, 1), (None, None), (None, 0)),
}


def call(kernel, out_shape, in_specs, flops, moved, exps):
    outs = jax.tree.map(lambda _: VMEM, out_shape)
    return pl.pallas_call(
        kernel,
        out_shape=out_shape,
        in_specs=in_specs,
        out_specs=outs,
        compiler_params=PARAMS,
        cost_estimate=pl.CostEstimate(flops=flops, bytes_accessed=moved, transcendentals=exps),
    )


def pack_kernel(key_ref, value_ref, query_ref, grad_ref, kv_ref, qg_ref, *scratch):
    buffers, sems = scratch[:4], scratch[4]
    rows, wide = key_ref.shape[0], query_ref.shape[0]
    targets = (
        kv_ref.at[pl.ds(0, rows)],
        kv_ref.at[pl.ds(rows, rows)],
        qg_ref.at[pl.ds(0, wide)],
        qg_ref.at[pl.ds(wide, wide)],
    )
    inward = [
        pltpu.make_async_copy(source, buffer, sems.at[index])
        for index, (source, buffer) in enumerate(
            zip((key_ref, value_ref, query_ref, grad_ref), buffers)
        )
    ]
    outward = [
        pltpu.make_async_copy(buffer, target, sems.at[4 + index])
        for index, (buffer, target) in enumerate(zip(buffers, targets))
    ]
    for copy in inward:
        copy.start()
    for copy, follow in zip(inward, outward):
        copy.wait()
        follow.start()
    for copy in outward:
        copy.wait()


def mask_kernel(table, lengths_ref, pattern_ref, bias_ref, lengths, pattern, sems):
    copies = [
        pltpu.make_async_copy(lengths_ref, lengths, sems.at[0]),
        pltpu.make_async_copy(pattern_ref, pattern, sems.at[1]),
    ]
    for copy in copies:
        copy.start()
    rows, wide = bias_ref.shape[1:]
    block = 128
    count = rows // block
    span = wide // count
    own = lax.axis_index("ctx")
    lane = lax.rem(lax.axis_index("head"), 2)
    valid, partners = [], []
    for pair in table:
        shift = jnp.where(lane == 0, pair[0] or 0, pair[1] or 0)
        exists = jnp.where(lane == 0, int(pair[0] is not None), int(pair[1] is not None))
        valid.append(jnp.where(own >= shift, exists, 0))
        partners.append(jnp.maximum(own - shift, 0))
    column = lax.broadcasted_iota(jnp.int32, (8, wide), 1)
    sub = lax.broadcasted_iota(jnp.int32, (8, wide), 0)
    pos = own * rows + lax.shift_right_logical(column, 1)
    for slot in range(SLOTS):
        pos = jnp.where(sub == slot + 1, partners[slot] * rows + column, pos)
    for copy in copies:
        copy.wait()

    def add_doc(index, carry):
        end, total = carry
        end = end + lengths[index]
        return end, total + jnp.where(pos >= end, 1.0, 0.0)

    docs = lax.fori_loop(
        0, lengths.shape[0], add_doc, (jnp.int32(0), jnp.zeros((8, wide), F32)), unroll=8
    )[1]
    query_doc = docs[0:1]
    query_pos = pos[0:1]
    down = lax.broadcasted_iota(jnp.int32, (block, span), 0)
    for slot, pair in enumerate(table):
        for kb in range(count):
            key_doc = docs[slot + 1 : slot + 2, kb * block : (kb + 1) * block]
            key_doc = jnp.broadcast_to(key_doc, (block, block)).T
            key_doc = jnp.concatenate([key_doc] * (span // block), axis=1)
            for qb in range(count):
                cols = slice(qb * span, (qb + 1) * span)
                open_pair = key_doc == query_doc[:, cols]
                if 0 in pair:
                    early = down + (partners[slot] * rows + kb * block) <= query_pos[:, cols]
                    open_pair = open_pair & early
                alive = pattern[qb, partners[slot] * count + kb] * valid[slot]
                live = jnp.where(alive == 1, 0.0, NEG)
                bias_ref[slot, kb * block : (kb + 1) * block, cols] = jnp.where(
                    open_pair, live, NEG
                )


def dot(a, b, dims):
    return lax.dot_general(a, b, (dims, ((), ())), preferred_element_type=F32)


NN = ((1,), (0,))
NT = ((1,), (1,))


def part_rows(ref, which):
    half = ref.shape[0] // 2
    return ref[which * half : (which + 1) * half, :]


def columns_of(ref, part):
    half = ref.shape[1] // 2
    return slice(part * half, (part + 1) * half)


def forward_kernel(slots, first, last, *refs):
    sides = refs[:2]
    bias_ref = refs[2]
    kv_refs = refs[3 : 3 + len(slots)]
    rest = refs[3 + len(slots) :]
    if not first:
        stat_in, out_in, *rest = rest
    stat_out, out_out = rest[:2]
    rows, wide = bias_ref.shape[1:]
    factor = math.log2(math.e) / math.sqrt(kv_refs[0].shape[1])
    values_t = [kv[rows:, :].T for kv in kv_refs]
    for part, side in enumerate(sides):
        cols = columns_of(stat_out, part)
        query = part_rows(side, 0)
        scores = [
            dot(kv[:rows, :], query, NT) * factor + bias_ref[slot]
            for kv, slot in zip(kv_refs, slots)
        ]
        top = functools.reduce(
            jnp.maximum, [jnp.max(piece, axis=0, keepdims=True) for piece in scores]
        )
        if not first:
            top = jnp.maximum(top, stat_in[0:1, cols])
        probs = [jnp.exp2(piece - top) for piece in scores]
        total = sum(jnp.sum(piece, axis=0, keepdims=True) for piece in probs)
        out = sum(dot(value, piece.astype(BF16), NN) for value, piece in zip(values_t, probs))
        if not first:
            fade = jnp.exp2(stat_in[0:1, cols] - top)
            total = total + stat_in[1:2, cols] * fade
            out = out + out_in[:, cols] * fade
        out_out[:, cols] = out
        stat_out[0:1, cols] = top
        stat_out[1:2, cols] = total
        if last:
            grad_t = part_rows(side, 1).T.astype(F32)
            stat_out[2:3, cols] = jnp.sum(grad_t * out, axis=0, keepdims=True)
            stat_out[3:4, cols] = jnp.zeros((1, wide), F32)
            if part == 1:
                rest[2][...] = (out / total).astype(BF16)
        else:
            stat_out[2:4, cols] = jnp.zeros((2, wide), F32)


def merged(stat_ref, other_stat_ref, part):
    cols = columns_of(stat_ref, part)
    other = columns_of(stat_ref, 1 - part)
    top_a, top_b = stat_ref[0:1, cols], other_stat_ref[0:1, other]
    top = jnp.maximum(top_a, top_b)
    fade_a, fade_b = jnp.exp2(top_a - top), jnp.exp2(top_b - top)
    total_b = other_stat_ref[1:2, other] * fade_b
    total = stat_ref[1:2, cols] * fade_a + total_b
    inner = stat_ref[2:3, cols] * fade_a + other_stat_ref[2:3, other] * fade_b
    return top + jnp.log2(total), inner / total, fade_a / total, total_b / total


def backward_kernel(slot, first, last, *refs):
    sides = refs[:2]
    bias_ref, kv_ref, stat_ref, other_stat_ref = refs[2:6]
    rest = refs[6:]
    rows = bias_ref.shape[1]
    dim = kv_ref.shape[1]
    if not first:
        query_in, rest = rest[0], rest[1:]
    grad_kv_ref, query_out = rest[:2]
    factor = math.log2(math.e) / math.sqrt(dim)
    scale = 1.0 / math.sqrt(dim)
    key = kv_ref[:rows, :]
    value = kv_ref[rows:, :]
    key_t = key.T
    grad_key = jnp.zeros((rows, dim), F32)
    grad_value = jnp.zeros((rows, dim), F32)
    for part, side in enumerate(sides):
        cols = columns_of(stat_ref, part)
        query, grad = part_rows(side, 0), part_rows(side, 1)
        norm, inner, _, _ = merged(stat_ref, other_stat_ref, part)
        scores = dot(key, query, NT) * factor + bias_ref[slot]
        probs = jnp.exp2(scores - norm)
        grad_value = grad_value + dot(probs.astype(BF16), grad, NN)
        grad_score = (probs * (dot(value, grad, NT) - inner)).astype(BF16)
        grad_key = grad_key + dot(grad_score, query, NN)
        grad_query = dot(key_t, grad_score, NN) * scale
        if not first:
            grad_query = query_in[:, cols] + grad_query
        query_out[:, cols] = grad_query
        if last and part == 1:
            rest[2][...] = grad_query.astype(BF16)
    grad_kv_ref[:rows, :] = (grad_key * scale).astype(BF16)
    grad_kv_ref[rows:, :] = grad_value.astype(BF16)


def finish_out_kernel(stat_ref, other_stat_ref, out_ref, got_ref, attn_ref):
    cols = columns_of(stat_ref, 0)
    _, _, weight_a, weight_b = merged(stat_ref, other_stat_ref, 0)
    out = out_ref[:, cols] * weight_a + got_ref[...].astype(F32) * weight_b
    attn_ref[...] = out.T.astype(BF16)


def finish_query_kernel(query_ref, got_ref, grad_ref):
    grad = query_ref[:, columns_of(query_ref, 0)] + got_ref[...].astype(F32)
    grad_ref[...] = grad.T.astype(BF16)


def sum_kernel(count, *refs):
    total = sum(ref[...].astype(F32) for ref in refs[:count]).astype(BF16)
    start = 0
    for ref in refs[count:]:
        ref[...] = total[start : start + ref.shape[0], :]
        start += ref.shape[0]


def local(queries, key_rows, value_rows, grad_out, doc_lengths, block_pattern):
    rows, heads, dim = queries.shape
    width = lax.axis_size("ctx")
    lanes = lax.axis_size("head")
    table = TABLES[width]
    edge = width * 3 // 4

    def lane_pairs(shifts, back):
        pairs = []
        for which, shift in enumerate(shifts):
            if shift is None:
                continue
            for source in range(width - shift):
                target = source + shift
                if (source < edge) != (target < edge):
                    continue
                for place in range(which, lanes, 2):
                    pair = (source * lanes + place, target * lanes + place)
                    pairs.append(pair[::-1] if back else pair)
        return pairs

    def swap_pairs(partner):
        return [
            (group * lanes + place, group * lanes + partner(place))
            for group in range(width)
            for place in range(lanes)
        ]

    def send(value, pairs):
        return lax.ppermute(value, AXES, pairs)

    near = swap_pairs(lambda place: place ^ 1)
    far = swap_pairs(lambda place: lanes - 1 - place)

    kv_shape = jax.ShapeDtypeStruct((2 * rows, dim), BF16)
    qg_shape = jax.ShapeDtypeStruct((2 * heads * rows, dim), BF16)
    own_kv, own_qg = pl.pallas_call(
        pack_kernel,
        out_shape=(kv_shape, qg_shape),
        in_specs=[HBM] * 4,
        out_specs=(HBM, HBM),
        scratch_shapes=[
            pltpu.VMEM((rows, dim), BF16),
            pltpu.VMEM((rows, dim), BF16),
            pltpu.VMEM((rows * heads, dim), BF16),
            pltpu.VMEM((rows * heads, dim), BF16),
            pltpu.SemaphoreType.DMA((8,)),
        ],
        compiler_params=pltpu.CompilerParams(vmem_limit_bytes=67043328),
    )(
        key_rows,
        value_rows,
        queries.reshape(rows * heads, dim),
        grad_out.reshape(rows * heads, dim),
    )
    held = [send(own_kv, lane_pairs(table[0], False))]
    other_qg = send(own_qg, near)
    for slot in range(1, SLOTS):
        held.append(send(own_kv, lane_pairs(table[slot], False)))

    bias = pl.pallas_call(
        functools.partial(mask_kernel, table),
        out_shape=jax.ShapeDtypeStruct((SLOTS, rows, heads * rows), F32),
        in_specs=[HBM, HBM],
        out_specs=VMEM,
        scratch_shapes=[
            pltpu.SMEM(doc_lengths.shape, jnp.int32),
            pltpu.SMEM(block_pattern.shape, jnp.int32),
            pltpu.SemaphoreType.DMA((2,)),
        ],
        compiler_params=PARAMS,
    )(doc_lengths, block_pattern)

    columns = 2 * heads * rows
    stat_shape = jax.ShapeDtypeStruct((4, columns), F32)
    wide_shape = jax.ShapeDtypeStruct((dim, columns), F32)
    unit = 2 * rows * columns * dim

    send_shape = jax.ShapeDtypeStruct((dim, heads * rows), BF16)

    def forward(slots, carry, last):
        first = carry is None
        kernel = functools.partial(forward_kernel, slots, first, last)
        args = [own_qg, other_qg, bias] + [held[s] for s in slots] + list(carry or ())
        return call(
            kernel,
            (stat_shape, wide_shape) + ((send_shape,) if last else ()),
            [VMEM] * len(args),
            2 * unit * len(slots),
            4 << 20,
            rows * columns * len(slots),
        )(*args)

    stat, out = forward((0, 1, 3), None, False)
    stat, out, other_out = forward((2,), (stat, out), True)
    other_stat = send(stat, near)
    got_out = send(other_out, near)

    returned = []
    query_grad = None
    for slot in range(SLOTS):
        first, last = slot == 0, slot == SLOTS - 1
        kernel = functools.partial(backward_kernel, slot, first, last)
        args = [own_qg, other_qg, bias, held[slot], stat, other_stat]
        if not first:
            args.append(query_grad)
        shapes = (kv_shape, wide_shape) + ((send_shape,) if last else ())
        results = call(
            kernel, shapes, [VMEM] * len(args), 5 * unit, 4 << 20, rows * columns
        )(*args)
        grad_kv, query_grad = results[:2]
        returned.append(send(grad_kv, lane_pairs(table[slot], True)))
    got_query = send(results[2], near)

    def add(pieces, shapes):
        kernel = functools.partial(sum_kernel, len(pieces))
        return call(kernel, shapes, [VMEM] * len(pieces), 0, 1 << 20, 0)(*pieces)

    total = add(returned, (kv_shape,))[0]
    total = add((total, send(total, far)), (kv_shape,))[0]
    key_shape = jax.ShapeDtypeStruct((rows, dim), BF16)
    grad_keys, grad_values = add((total, send(total, near)), (key_shape, key_shape))

    flat = jax.ShapeDtypeStruct((heads * rows, dim), BF16)
    attn = call(finish_out_kernel, flat, [VMEM] * 4, 0, 1 << 20, 0)(
        stat, other_stat, out, got_out
    )
    grad_q = call(finish_query_kernel, flat, [VMEM] * 2, 0, 1 << 20, 0)(
        query_grad, got_query
    )
    shape = (rows, heads, dim)
    return attn.reshape(shape), grad_q.reshape(shape), grad_keys, grad_values


def solution(mesh):
    wide, flat = P("ctx", "head", None), P("ctx", None)

    return jax.shard_map(
        local,
        mesh=mesh,
        in_specs=(wide, flat, flat, wide, P(), flat),
        out_specs=(wide, wide, flat, flat),
        check_vma=False,
    )
```

```python
import functools
import math

import jax
import jax.numpy as jnp
from jax import lax
from jax.experimental import pallas as pl
from jax.experimental.pallas import tpu as pltpu
from jax.sharding import PartitionSpec as P

NEG = -1e30
AXES = ("ctx", "head")
SLOTS = 4
VMEM = pl.BlockSpec(memory_space=pltpu.VMEM)
HBM = pl.BlockSpec(memory_space=pltpu.HBM)
PARAMS = pltpu.CompilerParams(vmem_limit_bytes=40 * 1024 * 1024)
F32 = jnp.float32
BF16 = jnp.bfloat16

TABLES = {
    128: ((64, 32), (8, 4), (16, 2), (1, 0)),
    16: ((8, 2), (4, 1), (None, None), (None, 0)),
}


def call(kernel, out_shape, in_specs, flops, moved, exps):
    outs = jax.tree.map(lambda _: VMEM, out_shape)
    return pl.pallas_call(
        kernel,
        out_shape=out_shape,
        in_specs=in_specs,
        out_specs=outs,
        compiler_params=PARAMS,
        cost_estimate=pl.CostEstimate(flops=flops, bytes_accessed=moved, transcendentals=exps),
    )


def pack_kernel(key_ref, value_ref, query_ref, grad_ref, kv_ref, qg_ref, *scratch):
    buffers, sems = scratch[:4], scratch[4]
    rows, wide = key_ref.shape[0], query_ref.shape[0]
    targets = (
        kv_ref.at[pl.ds(0, rows)],
        kv_ref.at[pl.ds(rows, rows)],
        qg_ref.at[pl.ds(0, wide)],
        qg_ref.at[pl.ds(wide, wide)],
    )
    inward = [
        pltpu.make_async_copy(source, buffer, sems.at[index])
        for index, (source, buffer) in enumerate(
            zip((key_ref, value_ref, query_ref, grad_ref), buffers)
        )
    ]
    outward = [
        pltpu.make_async_copy(buffer, target, sems.at[4 + index])
        for index, (buffer, target) in enumerate(zip(buffers, targets))
    ]
    for copy in inward:
        copy.start()
    for copy, follow in zip(inward, outward):
        copy.wait()
        follow.start()
    for copy in outward:
        copy.wait()


def mask_kernel(table, lengths_ref, pattern_ref, bias_ref, lengths, pattern, sems):
    copies = [
        pltpu.make_async_copy(lengths_ref, lengths, sems.at[0]),
        pltpu.make_async_copy(pattern_ref, pattern, sems.at[1]),
    ]
    for copy in copies:
        copy.start()
    rows, wide = bias_ref.shape[1:]
    block = 128
    count = rows // block
    span = wide // count
    own = lax.axis_index("ctx")
    lane = lax.rem(lax.axis_index("head"), 2)
    valid, partners = [], []
    for pair in table:
        shift = jnp.where(lane == 0, pair[0] or 0, pair[1] or 0)
        exists = jnp.where(lane == 0, int(pair[0] is not None), int(pair[1] is not None))
        valid.append(jnp.where(own >= shift, exists, 0))
        partners.append(jnp.maximum(own - shift, 0))
    column = lax.broadcasted_iota(jnp.int32, (8, wide), 1)
    sub = lax.broadcasted_iota(jnp.int32, (8, wide), 0)
    pos = own * rows + lax.shift_right_logical(column, 1)
    for slot in range(SLOTS):
        pos = jnp.where(sub == slot + 1, partners[slot] * rows + column, pos)
    for copy in copies:
        copy.wait()

    def add_doc(index, carry):
        end, total = carry
        end = end + lengths[index]
        return end, total + jnp.where(pos >= end, 1.0, 0.0)

    docs = lax.fori_loop(
        0, lengths.shape[0], add_doc, (jnp.int32(0), jnp.zeros((8, wide), F32)), unroll=8
    )[1]
    query_doc = docs[0:1]
    query_pos = pos[0:1]
    down = lax.broadcasted_iota(jnp.int32, (block, span), 0)
    for slot, pair in enumerate(table):
        for kb in range(count):
            key_doc = docs[slot + 1 : slot + 2, kb * block : (kb + 1) * block]
            key_doc = jnp.broadcast_to(key_doc, (block, block)).T
            key_doc = jnp.concatenate([key_doc] * (span // block), axis=1)
            for qb in range(count):
                cols = slice(qb * span, (qb + 1) * span)
                open_pair = key_doc == query_doc[:, cols]
                if 0 in pair:
                    early = down + (partners[slot] * rows + kb * block) <= query_pos[:, cols]
                    open_pair = open_pair & early
                alive = pattern[qb, partners[slot] * count + kb] * valid[slot]
                live = jnp.where(alive == 1, 0.0, NEG)
                bias_ref[slot, kb * block : (kb + 1) * block, cols] = jnp.where(
                    open_pair, live, NEG
                )


def dot(a, b, dims):
    return lax.dot_general(a, b, (dims, ((), ())), preferred_element_type=F32)


NN = ((1,), (0,))
NT = ((1,), (1,))


def part_rows(ref, which):
    half = ref.shape[0] // 2
    return ref[which * half : (which + 1) * half, :]


def columns_of(ref, part):
    half = ref.shape[1] // 2
    return slice(part * half, (part + 1) * half)


def forward_kernel(slots, first, last, *refs):
    sides = refs[:2]
    bias_ref = refs[2]
    kv_refs = refs[3 : 3 + len(slots)]
    rest = refs[3 + len(slots) :]
    if not first:
        stat_in, out_in, *rest = rest
    stat_out, out_out = rest[:2]
    rows, wide = bias_ref.shape[1:]
    factor = math.log2(math.e) / math.sqrt(kv_refs[0].shape[1])
    values_t = [kv[rows:, :].T for kv in kv_refs]
    for part, side in enumerate(sides):
        cols = columns_of(stat_out, part)
        query = part_rows(side, 0)
        scores = [
            dot(kv[:rows, :], query, NT) * factor + bias_ref[slot]
            for kv, slot in zip(kv_refs, slots)
        ]
        top = functools.reduce(
            jnp.maximum, [jnp.max(piece, axis=0, keepdims=True) for piece in scores]
        )
        if not first:
            top = jnp.maximum(top, stat_in[0:1, cols])
        probs = [jnp.exp2(piece - top) for piece in scores]
        total = sum(jnp.sum(piece, axis=0, keepdims=True) for piece in probs)
        out = sum(dot(value, piece.astype(BF16), NN) for value, piece in zip(values_t, probs))
        if not first:
            fade = jnp.exp2(stat_in[0:1, cols] - top)
            total = total + stat_in[1:2, cols] * fade
            out = out + out_in[:, cols] * fade
        out_out[:, cols] = out
        stat_out[0:1, cols] = top
        stat_out[1:2, cols] = total
        if last:
            grad_t = part_rows(side, 1).T.astype(F32)
            stat_out[2:3, cols] = jnp.sum(grad_t * out, axis=0, keepdims=True)
            stat_out[3:4, cols] = jnp.zeros((1, wide), F32)
            if part == 1:
                rest[2][...] = (out / total).astype(BF16)
        else:
            stat_out[2:4, cols] = jnp.zeros((2, wide), F32)


def merged(stat_ref, other_stat_ref, part):
    cols = columns_of(stat_ref, part)
    other = columns_of(stat_ref, 1 - part)
    top_a, top_b = stat_ref[0:1, cols], other_stat_ref[0:1, other]
    top = jnp.maximum(top_a, top_b)
    fade_a, fade_b = jnp.exp2(top_a - top), jnp.exp2(top_b - top)
    total_b = other_stat_ref[1:2, other] * fade_b
    total = stat_ref[1:2, cols] * fade_a + total_b
    inner = stat_ref[2:3, cols] * fade_a + other_stat_ref[2:3, other] * fade_b
    return top + jnp.log2(total), inner / total, fade_a / total, total_b / total


def backward_kernel(slots, first, last, *refs):
    sides = refs[:2]
    bias_ref = refs[2]
    kv_refs = refs[3 : 3 + len(slots)]
    stat_ref, other_stat_ref, *rest = refs[3 + len(slots) :]
    rows = bias_ref.shape[1]
    dim = kv_refs[0].shape[1]
    if not first:
        query_in, *rest = rest
    grad_refs, rest = rest[: len(slots)], rest[len(slots) :]
    query_out = rest[0]
    factor = math.log2(math.e) / math.sqrt(dim)
    scale = 1.0 / math.sqrt(dim)
    grad_keys = [jnp.zeros((rows, dim), F32) for _ in slots]
    grad_values = [jnp.zeros((rows, dim), F32) for _ in slots]
    for part, side in enumerate(sides):
        cols = columns_of(stat_ref, part)
        query, grad = part_rows(side, 0), part_rows(side, 1)
        norm, inner, _, _ = merged(stat_ref, other_stat_ref, part)
        grad_query = 0.0
        for place, slot in enumerate(slots):
            key, value = kv_refs[place][:rows, :], kv_refs[place][rows:, :]
            scores = dot(key, query, NT) * factor + bias_ref[slot]
            probs = jnp.exp2(scores - norm)
            grad_values[place] = grad_values[place] + dot(probs.astype(BF16), grad, NN)
            grad_score = (probs * (dot(value, grad, NT) - inner)).astype(BF16)
            grad_keys[place] = grad_keys[place] + dot(grad_score, query, NN)
            grad_query = grad_query + dot(key.T, grad_score, NN)
        grad_query = grad_query * scale
        if not first:
            grad_query = query_in[:, cols] + grad_query
        query_out[:, cols] = grad_query
        if last and part == 1:
            rest[1][...] = grad_query.astype(BF16)
    for ref, grad_key, grad_value in zip(grad_refs, grad_keys, grad_values):
        ref[:rows, :] = (grad_key * scale).astype(BF16)
        ref[rows:, :] = grad_value.astype(BF16)


def finish_out_kernel(stat_ref, other_stat_ref, out_ref, got_ref, attn_ref):
    cols = columns_of(stat_ref, 0)
    _, _, weight_a, weight_b = merged(stat_ref, other_stat_ref, 0)
    out = out_ref[:, cols] * weight_a + got_ref[...].astype(F32) * weight_b
    attn_ref[...] = out.T.astype(BF16)


def finish_query_kernel(query_ref, got_ref, grad_ref):
    grad = query_ref[:, columns_of(query_ref, 0)] + got_ref[...].astype(F32)
    grad_ref[...] = grad.T.astype(BF16)


def sum_kernel(count, *refs):
    total = sum(ref[...].astype(F32) for ref in refs[:count]).astype(BF16)
    start = 0
    for ref in refs[count:]:
        ref[...] = total[start : start + ref.shape[0], :]
        start += ref.shape[0]


def local(queries, key_rows, value_rows, grad_out, doc_lengths, block_pattern):
    rows, heads, dim = queries.shape
    width = lax.axis_size("ctx")
    lanes = lax.axis_size("head")
    table = TABLES[width]
    edge = width * 3 // 4

    def lane_pairs(shifts, back):
        pairs = []
        for which, shift in enumerate(shifts):
            if shift is None:
                continue
            for source in range(width - shift):
                target = source + shift
                if (source < edge) != (target < edge):
                    continue
                for place in range(which, lanes, 2):
                    pair = (source * lanes + place, target * lanes + place)
                    pairs.append(pair[::-1] if back else pair)
        return pairs

    def swap_pairs(partner):
        return [
            (group * lanes + place, group * lanes + partner(place))
            for group in range(width)
            for place in range(lanes)
        ]

    def send(value, pairs):
        return lax.ppermute(value, AXES, pairs)

    near = swap_pairs(lambda place: place ^ 1)
    far = swap_pairs(lambda place: lanes - 1 - place)

    kv_shape = jax.ShapeDtypeStruct((2 * rows, dim), BF16)
    qg_shape = jax.ShapeDtypeStruct((2 * heads * rows, dim), BF16)
    own_kv, own_qg = pl.pallas_call(
        pack_kernel,
        out_shape=(kv_shape, qg_shape),
        in_specs=[HBM] * 4,
        out_specs=(HBM, HBM),
        scratch_shapes=[
            pltpu.VMEM((rows, dim), BF16),
            pltpu.VMEM((rows, dim), BF16),
            pltpu.VMEM((rows * heads, dim), BF16),
            pltpu.VMEM((rows * heads, dim), BF16),
            pltpu.SemaphoreType.DMA((8,)),
        ],
        compiler_params=pltpu.CompilerParams(vmem_limit_bytes=67043328),
    )(
        key_rows,
        value_rows,
        queries.reshape(rows * heads, dim),
        grad_out.reshape(rows * heads, dim),
    )
    held = [send(own_kv, lane_pairs(table[0], False))]
    other_qg = send(own_qg, near)
    for slot in range(1, SLOTS):
        held.append(send(own_kv, lane_pairs(table[slot], False)))

    bias = pl.pallas_call(
        functools.partial(mask_kernel, table),
        out_shape=jax.ShapeDtypeStruct((SLOTS, rows, heads * rows), F32),
        in_specs=[HBM, HBM],
        out_specs=VMEM,
        scratch_shapes=[
            pltpu.SMEM(doc_lengths.shape, jnp.int32),
            pltpu.SMEM(block_pattern.shape, jnp.int32),
            pltpu.SemaphoreType.DMA((2,)),
        ],
        compiler_params=PARAMS,
    )(doc_lengths, block_pattern)

    columns = 2 * heads * rows
    stat_shape = jax.ShapeDtypeStruct((4, columns), F32)
    wide_shape = jax.ShapeDtypeStruct((dim, columns), F32)
    unit = 2 * rows * columns * dim

    send_shape = jax.ShapeDtypeStruct((dim, heads * rows), BF16)

    def forward(slots, carry, last):
        first = carry is None
        kernel = functools.partial(forward_kernel, slots, first, last)
        args = [own_qg, other_qg, bias] + [held[s] for s in slots] + list(carry or ())
        return call(
            kernel,
            (stat_shape, wide_shape) + ((send_shape,) if last else ()),
            [VMEM] * len(args),
            2 * unit * len(slots),
            4 << 20,
            rows * columns * len(slots),
        )(*args)

    stat, out = forward((0, 1, 3), None, False)
    stat, out, other_out = forward((2,), (stat, out), True)
    other_stat = send(stat, near)
    got_out = send(other_out, near)

    returned = []
    query_grad = None
    for slots in ((0,), (1,), (2, 3)):
        first, last = slots[0] == 0, slots[-1] == SLOTS - 1
        kernel = functools.partial(backward_kernel, slots, first, last)
        args = [own_qg, other_qg, bias] + [held[s] for s in slots] + [stat, other_stat]
        if not first:
            args.append(query_grad)
        shapes = (kv_shape,) * len(slots) + (wide_shape,) + ((send_shape,) if last else ())
        results = call(
            kernel, shapes, [VMEM] * len(args), 5 * unit * len(slots), 8 << 20, rows * columns * len(slots)
        )(*args)
        query_grad = results[len(slots)]
        for slot, grad_kv in zip(slots, results):
            returned.append(send(grad_kv, lane_pairs(table[slot], True)))
    got_query = send(results[3], near)

    def add(pieces, shapes):
        kernel = functools.partial(sum_kernel, len(pieces))
        return call(kernel, shapes, [VMEM] * len(pieces), 0, 1 << 20, 0)(*pieces)

    total = add(returned, (kv_shape,))[0]
    total = add((total, send(total, near)), (kv_shape,))[0]
    key_shape = jax.ShapeDtypeStruct((rows, dim), BF16)
    grad_keys, grad_values = add((total, send(total, far)), (key_shape, key_shape))

    flat = jax.ShapeDtypeStruct((heads * rows, dim), BF16)
    attn = call(finish_out_kernel, flat, [VMEM] * 4, 0, 1 << 20, 0)(
        stat, other_stat, out, got_out
    )
    grad_q = call(finish_query_kernel, flat, [VMEM] * 2, 0, 1 << 20, 0)(
        query_grad, got_query
    )
    shape = (rows, heads, dim)
    return attn.reshape(shape), grad_q.reshape(shape), grad_keys, grad_values


def solution(mesh):
    wide, flat = P("ctx", "head", None), P("ctx", None)

    return jax.shard_map(
        local,
        mesh=mesh,
        in_specs=(wide, flat, flat, wide, P(), flat),
        out_specs=(wide, wide, flat, flat),
        check_vma=False,
    )
```
